256 devices in a mesh: row: 32 (over x, y, z_hi), rep: 8 (over z_lo, core).
Axes of the slice: x: 4, y: 4, z: 8 (z_hi: 2, z_lo: 4; z = z_hi * 4 + z_lo), core: 2. Of those that a mesh axis runs over, the one named last changes fastest.
Arguments:
- features: bfloat16 [65536, 256], P(('row', 'rep')), may hold values from -24 to 24
- weight: bfloat16 [256, 256], replicated, may hold values from -2 to 2
- degrees: int32 [65536], P(('row', 'rep')), may hold values from 1 to 16416, as said below
- cotangent: bfloat16 [65536, 256], P(('row', 'rep')), may hold values from -6 to 6
- tile_cols: int32 [4096, 16], P(('row', 'rep')), may hold values from 0 to 63, as said below
- list_len: int32 [4096], P(('row', 'rep')), may hold values from 1 to 16, as said below
- tiles: bfloat16 [4096, 16, 128, 128], P(('row', 'rep')), may hold values from 0 to 1, as said below
Outputs:
- activated: bfloat16 [65536, 256], P(('row', 'rep'))
- grad_x: bfloat16 [65536, 256], P(('row', 'rep'))
- grad_w: float32 [256, 256], P('row')
The draws below stay inside these ranges and needn't reach their ends.
Inputs may be any that keep to these rules, and one draw needn't show every extreme that they name: `tile_cols`: within one list the 16 column tiles are distinct. `list_len`: on every device some list has exactly 16 live slots. `tiles`: entries are 0 or 1. `degrees`: each node's degree exceeds the number of ones in its row of A; some node has exactly the largest value.
All inputs are finite; a program needn't handle non-finite values.
Results may differ from the reference program's by a relative error of at most 0.006.
Values may be sent and summed in bfloat16 or wider, within the bound.
No kernel may reach another device: no remote copies, remote signals or barrier semaphores. Data moves between devices by JAX's collectives and lax.ppermute only.
A program may use at most 128 MiB of HBM per device.

```python
import math
import jax
import jax.numpy as jnp
from jax import lax

F = 256
TILE = 128
KR = 16
SHARE = 256
BLOCK_ROWS = 2048
NODES = 65536
TROWS = 16
GCOLS = 64
LISTS = 4096
N_ROW = 32
N_REP = 8


def draw_tile_cols(key, part):
    key_list = jax.random.split(key, LISTS)

    def one_list(sub_key):
        return jax.random.permutation(sub_key, GCOLS)[:KR].astype(jnp.int32)
    return jax.vmap(one_list)(key_list)


def lengths_from(key):
    device_count = LISTS // TROWS
    own_key = jax.random.fold_in(key, 101)
    key_level, key_len, key_pick = jax.random.split(own_key, 3)
    load_level = jax.random.randint(key_level, (device_count, 1), 1, 5)
    most_len = jnp.maximum(load_level * KR // 4, 1)
    lengths = jax.random.randint(key_len, (device_count, TROWS), 1, most_len + 1)
    chosen = jax.random.randint(key_pick, (device_count, 1), 0, TROWS)
    positions = jnp.arange(TROWS)[None, :]
    lengths = jnp.where(positions == chosen, KR, lengths)
    return lengths.astype(jnp.int32)


def device_pattern(key, device_index):
    own_key = jax.random.fold_in(jax.random.fold_in(key, 202), device_index)
    key_density, key_bits = jax.random.split(own_key)
    density = jax.random.randint(key_density, (TROWS, KR, 1, 1), 15, 61)
    noise = jax.random.randint(key_bits, (TROWS, KR, TILE, TILE), 0, 1000)
    return jnp.where(noise < density, 1, 0).astype(jnp.int32)


def draw_list_len(key, part):
    return lengths_from(key).reshape(LISTS)


def draw_tiles(key, part):
    device_count = LISTS // TROWS

    def one_device(device_index):
        return device_pattern(key, device_index).astype(jnp.float32).astype(jnp.bfloat16)
    drawn = lax.map(one_device, jnp.arange(device_count))
    return drawn.reshape(LISTS, KR, TILE, TILE)


def draw_degrees(key, part):
    device_count = LISTS // TROWS
    lengths = lengths_from(key)

    def one_device(device_index):
        pattern = device_pattern(key, device_index)
        live = (jnp.arange(KR)[None, :] < lengths[device_index][:, None]).astype(jnp.int32)
        return jnp.sum(pattern.sum(axis=3) * live[:, :, None], axis=1)
    counts = lax.map(one_device, jnp.arange(device_count))
    counts = counts.reshape(N_ROW, N_REP, TROWS, TILE).sum(axis=1).reshape(NODES)
    extra = jax.random.randint(jax.random.fold_in(key, 303), (NODES,), 1, 33)
    top_degree = N_REP * KR * TILE + 32
    chosen = jax.random.randint(jax.random.fold_in(key, 404), (), 0, NODES)
    degrees = jnp.where(jnp.arange(NODES) == chosen, top_degree, counts + extra)
    return degrees.astype(jnp.int32)


def spiked(entries, key, source, target, parts, factor):
    owner, partner = [(jnp.arange(entries.shape[position]) // (entries.shape[position] // parts)).reshape([-1 if axis == position else 1 for axis in range(entries.ndim)]) for position in (source, target)]
    chosen = jax.random.permutation(key, parts)[partner]
    strong = (owner == chosen) | (owner == (partner + parts // 2) % parts)
    return jnp.where(strong, factor * entries, entries)


def level_of(key, extent, shards, least, high):
    level, own = 1.0, jax.random.fold_in(key, 6)
    for axis_at, parts in shards:
        heights = jnp.exp(jax.random.uniform(jax.random.fold_in(own, axis_at), (parts,), jnp.float32, least / len(shards), high / len(shards)))
        level = level * jnp.repeat(heights, extent[axis_at] // parts).reshape([-1 if axis == axis_at else 1 for axis in range(len(extent))])
    return level


def scatter_about(rng, shape, deviation, most, pieces=(), kind=jnp.bfloat16):
    array = deviation * jax.random.normal(rng, shape, jnp.float32)
    if pieces:
        array = array * level_of(rng, shape, pieces, -0.22, 0.18)
    return jnp.clip(array, -most, most).astype(kind)


def heavy_noise(key, extent, deviation, most, pieces, heavy, kind=jnp.bfloat16):
    values = deviation * jax.random.normal(key, extent, jnp.float32)
    if pieces:
        values = values * level_of(key, extent, pieces, -0.22, 0.18)
    return jnp.clip(spiked(values, jax.random.fold_in(key, 3), *heavy), -most, most).astype(kind)


def setup_inputs(seed: int = 0) -> dict:
    arg_keys = jax.random.split(jax.random.key(seed), 8)
    return {
        "features": heavy_noise(arg_keys[0], (NODES, F), 1.0, 24.0, ((0, 256),), (0, 1, 256, 6.0)),
        "weight": scatter_about(arg_keys[1], (F, F), (F // 32) ** -0.5, 2.0),
        "degrees": draw_degrees(jax.random.fold_in(arg_keys[7], 71), 0),
        "cotangent": scatter_about(arg_keys[3], (NODES, F), 1.0, 6.0, ((0, 256),)),
        "tile_cols": draw_tile_cols(jax.random.fold_in(arg_keys[7], 71), 0),
        "list_len": draw_list_len(jax.random.fold_in(arg_keys[7], 71), 0),
        "tiles": draw_tiles(jax.random.fold_in(arg_keys[7], 71), 0),
    }


def reference(features, weight, degrees, cotangent, tile_cols, list_len, tiles):
    width = features.shape[1]
    inv_root = 1.0 / jnp.sqrt(degrees.astype(jnp.float32))
    scaled = (features.astype(jnp.float32) * inv_root[:, None]).astype(jnp.bfloat16)
    section_view = scaled.reshape(N_ROW, N_REP, SHARE, width).transpose(1, 0, 2, 3).reshape(N_REP, GCOLS, TILE, width)
    slot_ids = jnp.arange(KR).astype(jnp.int32)
    live_slots = (slot_ids[None, :] < list_len[:, None]).astype(jnp.bfloat16)
    list_ids = jnp.arange(LISTS).astype(jnp.int32)

    def masked_tiles(list_index):
        return tiles[list_index] * live_slots[list_index][:, None, None]

    def forward_list(list_index):
        rep_group = list_index // TROWS % N_REP
        pattern = masked_tiles(list_index)
        row_tiles = pattern.transpose(1, 0, 2).reshape(TILE, KR * TILE)
        picked = section_view[rep_group][tile_cols[list_index]].reshape(KR * TILE, width)
        return jnp.dot(row_tiles, picked, preferred_element_type=jnp.float32)
    partial_value = lax.map(forward_list, list_ids)
    aggregate = partial_value.reshape(N_ROW, N_REP, BLOCK_ROWS, width).sum(axis=1).reshape(NODES, width)
    pooled = (aggregate * inv_root[:, None]).astype(jnp.bfloat16)
    preact = jnp.dot(pooled, weight, preferred_element_type=jnp.float32)
    activated = jax.nn.silu(preact).astype(jnp.bfloat16)
    sigmoid_val = jax.nn.sigmoid(preact)
    grad_pre = (cotangent.astype(jnp.float32) * sigmoid_val * (1.0 + preact * (1.0 - sigmoid_val))).astype(jnp.bfloat16)
    grad_w = lax.dot_general(pooled, grad_pre, (((0,), (0,)), ((), ())), preferred_element_type=jnp.float32) * (1.0 / math.sqrt(NODES))
    back_rows = (lax.dot_general(grad_pre, weight, (((1,), (1,)), ((), ())), preferred_element_type=jnp.float32) * inv_root[:, None]).astype(jnp.bfloat16)
    back_tiles = back_rows.reshape(N_ROW * TROWS, TILE, width)

    def backward_list(running, list_index):
        row_block = list_index // (N_REP * TROWS)
        rep_group = list_index // TROWS % N_REP
        tile_row = list_index % TROWS
        pattern = masked_tiles(list_index)
        col_tiles = pattern.transpose(0, 2, 1).reshape(KR * TILE, TILE)
        block_rows = back_tiles[row_block * TROWS + tile_row]
        contrib = jnp.dot(col_tiles, block_rows, preferred_element_type=jnp.float32).reshape(KR, TILE, width)
        running = running.at[rep_group, tile_cols[list_index]].add(contrib)
        return (running, None)
    zero_total = jnp.zeros((N_REP, GCOLS, TILE, width), jnp.float32)
    col_total, _ = lax.scan(backward_list, zero_total, list_ids)
    transposed = col_total.reshape(N_REP, N_ROW, SHARE, width).transpose(1, 0, 2, 3).reshape(NODES, width)
    grad_x = (transposed * inv_root[:, None]).astype(jnp.bfloat16)
    return (activated, grad_x, grad_w)
```

```python
import math

import jax
import jax.numpy as jnp
from jax import lax
from jax.experimental import pallas as pl
from jax.experimental.pallas import tpu as pltpu
from jax.sharding import PartitionSpec as P


GROUP = 4


def live_tiles(tiles_ref, first, count):
    picked = [tiles_ref[0, first]]
    for slot in range(first + 1, first + GROUP):
        tile = tiles_ref[0, slot]
        picked.append(jnp.where(slot < count, tile, jnp.zeros_like(tile)))
    return jnp.concatenate(picked, axis=1)


def forward_kernel(cols_ref, len_ref, tiles_ref, section_ref, out_ref):
    row = pl.program_id(0)
    count = len_ref[row]
    out_ref[...] = jnp.zeros_like(out_ref)
    for first in range(0, tiles_ref.shape[1], GROUP):

        @pl.when(first < count)
        def _(first=first):
            picked = jnp.concatenate(
                [section_ref[cols_ref[row, first + step]] for step in range(GROUP)], axis=0
            )
            out_ref[...] += jnp.dot(
                live_tiles(tiles_ref, first, count),
                picked,
                preferred_element_type=jnp.float32,
            )


def backward_kernel(cols_ref, len_ref, tiles_ref, back_ref, out_ref):
    row = pl.program_id(0)
    count = len_ref[row]
    tile = tiles_ref.shape[2]

    @pl.when(row == 0)
    def _():
        out_ref[...] = jnp.zeros_like(out_ref)

    for first in range(0, tiles_ref.shape[1], GROUP):

        @pl.when(first < count)
        def _(first=first):
            contrib = lax.dot_general(
                live_tiles(tiles_ref, first, count),
                back_ref[...],
                (((0,), (0,)), ((), ())),
                preferred_element_type=jnp.float32,
            )
            for step in range(GROUP):
                col = cols_ref[row, first + step]
                out_ref[col] += contrib[step * tile : (step + 1) * tile]


def spmm(kernel, tile_cols, list_len, tiles, dense, dense_spec, out_shape, out_spec):
    rows, slots, tile, _ = tiles.shape
    width = dense.shape[-1]
    return pl.pallas_call(
        kernel,
        out_shape=out_shape,
        grid_spec=pltpu.PrefetchScalarGridSpec(
            num_scalar_prefetch=2,
            grid=(rows,),
            in_specs=[
                pl.BlockSpec((1, slots, tile, tile), lambda i, *_: (i, 0, 0, 0)),
                dense_spec,
            ],
            out_specs=out_spec,
        ),
        cost_estimate=pl.CostEstimate(
            flops=2 * rows * slots * tile * tile * width,
            bytes_accessed=2 * tiles.size + 2 * dense.size + 4 * math.prod(out_shape.shape),
            transcendentals=0,
        ),
    )(tile_cols, list_len, tiles, dense)


def on_device(features, weight, degrees, cotangent, tile_cols, list_len, tiles):
    node_rows, feat_width = features.shape
    tile_rows = tiles.shape[0]
    tile_size = tiles.shape[2]
    inv_root = 1.0 / jnp.sqrt(degrees.astype(jnp.float32))
    scaled_feats = (features.astype(jnp.float32) * inv_root[:, None]).astype(jnp.bfloat16)
    gathered = lax.all_gather(scaled_feats, "row", axis=0, tiled=True)
    section_tiles = gathered.reshape(-1, tile_size, feat_width)
    col_tiles = section_tiles.shape[0]
    partial_value = spmm(
        forward_kernel,
        tile_cols,
        list_len,
        tiles,
        section_tiles,
        pl.BlockSpec(section_tiles.shape, lambda i, *_: (0, 0, 0)),
        jax.ShapeDtypeStruct((tile_rows * tile_size, feat_width), jnp.float32),
        pl.BlockSpec((tile_size, feat_width), lambda i, *_: (i, 0)),
    )
    summed = lax.psum_scatter(partial_value, "rep", scatter_dimension=0, tiled=True)
    pooled = (summed * inv_root[:, None]).astype(jnp.bfloat16)
    preact = jnp.dot(pooled, weight, preferred_element_type=jnp.float32)
    activated = jax.nn.silu(preact).astype(jnp.bfloat16)
    sigmoid_val = jax.nn.sigmoid(preact)
    grad_pre = (
        cotangent.astype(jnp.float32) * sigmoid_val * (1.0 + preact * (1.0 - sigmoid_val))
    ).astype(jnp.bfloat16)
    weight_local = lax.dot_general(
        pooled, grad_pre, (((0,), (0,)), ((), ())), preferred_element_type=jnp.float32
    )
    back_rows = lax.dot_general(
        grad_pre, weight, (((1,), (1,)), ((), ())), preferred_element_type=jnp.float32
    )
    back_rows = (back_rows * inv_root[:, None]).astype(jnp.bfloat16)
    back_block = lax.all_gather(back_rows, "rep", axis=0, tiled=True)
    col_shape = (col_tiles, tile_size, feat_width)
    col_sums = spmm(
        backward_kernel,
        tile_cols,
        list_len,
        tiles,
        back_block,
        pl.BlockSpec((tile_size, feat_width), lambda i, *_: (i, 0)),
        jax.ShapeDtypeStruct(col_shape, jnp.float32),
        pl.BlockSpec(col_shape, lambda i, *_: (0, 0, 0)),
    )
    reduced_cols = lax.psum_scatter(
        col_sums.reshape(-1, feat_width), "row", scatter_dimension=0, tiled=True
    )
    node_total = node_rows * lax.axis_size("row") * lax.axis_size("rep")
    weight_norm = 1.0 / math.sqrt(node_total)
    rows_each = feat_width // lax.axis_size("row")
    weight_all = lax.psum(weight_local, ("row", "rep"))
    weight_rows = lax.dynamic_slice_in_dim(
        weight_all, lax.axis_index("row") * rows_each, rows_each, 0
    )
    grad_x = (reduced_cols * inv_root[:, None]).astype(jnp.bfloat16)
    return (activated, grad_x, weight_rows * weight_norm)


def solution(mesh):
    return jax.shard_map(
        on_device,
        mesh=mesh,
        in_specs=(
            P(("row", "rep"), None),
            P(),
            P(("row", "rep")),
            P(("row", "rep"), None),
            P(("row", "rep"), None),
            P(("row", "rep")),
            P(("row", "rep"), None, None, None),
        ),
        out_specs=(P(("row", "rep"), None), P(("row", "rep"), None), P("row", None)),
        check_vma=False,
    )
```
